32 devices in a mesh: bx: 8 (over y, x, core), by: 4 (over z).
Axes of the slice: x: 2, y: 2, z: 4, core: 2. Of those that a mesh axis runs over, the one named last changes fastest.
Arguments:
- right_sides: float32 [8, 4, 128, 768], P('bx', 'by'), may hold values from -6 to 6
- skeleton_order: int32 [8, 4, 4, 768], P('bx', 'by'), may hold values from 0 to 767, as said below
- interp_first: float32 [8, 4, 384, 384], P('bx', 'by'), may hold values from -0.15625 to 0.15625
- interp_second: float32 [8, 4, 384, 192], P('bx', 'by'), may hold values from -0.15625 to 0.15625
- interp_third: float32 [8, 4, 384, 96], P('bx', 'by'), may hold values from -0.15625 to 0.15625
- interp_fourth: float32 [8, 4, 384, 48], P('bx', 'by'), may hold values from -0.15625 to 0.15625
- inverse_first: float32 [8, 4, 384, 384], P('bx', 'by'), may hold values from -0.25 to 0.25
- inverse_second: float32 [8, 4, 384, 192], P('bx', 'by'), may hold values from -0.25 to 0.25
- inverse_third: float32 [8, 4, 384, 96], P('bx', 'by'), may hold values from -0.25 to 0.25
- inverse_fourth: float32 [8, 4, 384, 48], P('bx', 'by'), may hold values from -0.25 to 0.25
- couple_first: float32 [8, 4, 5, 384, 384], P('bx', 'by'), may hold values from -0.09375 to 0.09375
- couple_second: float32 [8, 4, 5, 384, 192], P('bx', 'by'), may hold values from -0.09375 to 0.09375
- couple_third: float32 [8, 4, 5, 384, 96], P('bx', 'by'), may hold values from -0.09375 to 0.09375
- couple_fourth: float32 [8, 4, 5, 384, 48], P('bx', 'by'), may hold values from -0.09375 to 0.09375
- root_inverse: float32 [8, 4, 384, 48], P('bx', 'by'), may hold values from -0.21875 to 0.21875
Outputs:
- solution: float32 [8, 4, 128, 768], P('bx', 'by')
The draws below stay inside these ranges and needn't reach their ends.
Inputs may be any that keep to these rules, and one draw needn't show every extreme that they name: For every fine box and level l, skeleton_order[i, j, l, :] is a permutation of 0 to 767, the same at all fine boxes of one level-l box.
All inputs are finite; a program needn't handle non-finite values.
Results may differ from the reference program's by a relative error of at most 0.0003.
Values sent between devices are 32-bit elements; how exact they have to be, the bound alone decides.
A program may use at most 128 MiB of HBM per device.

```python
import jax
import jax.numpy as jnp
from jax import lax

SKEL = 384
BOX = 768
NRHS = 128
BOXES_X = 8
BOXES_Y = 4


def draw_skeleton_order(key, part):
    stacked = []
    for level_index, extent in enumerate(((1, 1), (1, 2), (2, 2), (2, 4))):
        group_x, group_y = extent
        box_count = BOXES_X // group_x * (BOXES_Y // group_y)
        subkeys = jax.random.split(jax.random.fold_in(key, level_index + 11), box_count)
        shuffles = jax.vmap(lambda subkey: jax.random.permutation(subkey, BOX))(subkeys)
        layout = shuffles.reshape(BOXES_X // group_x, BOXES_Y // group_y, BOX)
        layout = jnp.repeat(jnp.repeat(layout, group_x, axis=0), group_y, axis=1)
        stacked.append(layout)
    return jnp.stack(stacked, axis=2).astype(jnp.int32)


def level_of(rng, shape, shards, low, high):
    def one(axis_at, shards_of):
        steps = jax.random.uniform(jax.random.fold_in(jax.random.fold_in(rng, 6), axis_at), (shards_of,), jnp.float32, low / len(shards), high / len(shards))
        return jnp.repeat(jnp.exp(steps), shape[axis_at] // shards_of).reshape((-1,) + (1,) * (len(shape) - axis_at - 1))

    loudness = one(*shards[0])
    for cut in shards[1:]:
        loudness = loudness * one(*cut)
    return loudness


def scatter_about(stream_key, shape, deviation, bound, cuts=(), held_as=jnp.bfloat16):
    values = deviation * jax.random.normal(stream_key, shape, jnp.float32)
    if cuts:
        values = values * level_of(stream_key, shape, cuts, -0.22, 0.18)
    return jnp.clip(values, -bound, bound).astype(held_as)


def setup_inputs(seed: int = 0) -> dict:
    keys = jax.random.split(jax.random.key(seed), 16)
    return {
        "right_sides": scatter_about(keys[0], (BOXES_X, BOXES_Y, NRHS, BOX), 1.0, 6.0, ((0, 8), (1, 4)), jnp.float32),
        "skeleton_order": draw_skeleton_order(jax.random.fold_in(keys[15], 71), 0),
        "interp_first": scatter_about(keys[2], (BOXES_X, BOXES_Y, SKEL, SKEL), (4 * SKEL) ** -0.5, 0.15625, ((0, 8), (1, 4)), jnp.float32),
        "interp_second": scatter_about(keys[3], (BOXES_X, BOXES_Y, SKEL, SKEL // 2), (4 * SKEL) ** -0.5, 0.15625, ((0, 8), (1, 4)), jnp.float32),
        "interp_third": scatter_about(keys[4], (BOXES_X, BOXES_Y, SKEL, SKEL // 4), (4 * SKEL) ** -0.5, 0.15625, ((0, 8), (1, 4)), jnp.float32),
        "interp_fourth": scatter_about(keys[5], (BOXES_X, BOXES_Y, SKEL, SKEL // 8), (4 * SKEL) ** -0.5, 0.15625, ((0, 8), (1, 4)), jnp.float32),
        "inverse_first": scatter_about(keys[6], (BOXES_X, BOXES_Y, SKEL, SKEL), (SKEL * 5 // 4) ** -0.5, 0.25, ((0, 8), (1, 4)), jnp.float32),
        "inverse_second": scatter_about(keys[7], (BOXES_X, BOXES_Y, SKEL, SKEL // 2), (SKEL * 5 // 4) ** -0.5, 0.25, ((0, 8), (1, 4)), jnp.float32),
        "inverse_third": scatter_about(keys[8], (BOXES_X, BOXES_Y, SKEL, SKEL // 4), (SKEL * 5 // 4) ** -0.5, 0.25, ((0, 8), (1, 4)), jnp.float32),
        "inverse_fourth": scatter_about(keys[9], (BOXES_X, BOXES_Y, SKEL, SKEL // 8), (SKEL * 5 // 4) ** -0.5, 0.25, ((0, 8), (1, 4)), jnp.float32),
        "couple_first": scatter_about(keys[10], (BOXES_X, BOXES_Y, 5, SKEL, SKEL), (10 * SKEL) ** -0.5, 0.09375, ((0, 8), (1, 4)), jnp.float32),
        "couple_second": scatter_about(keys[11], (BOXES_X, BOXES_Y, 5, SKEL, SKEL // 2), (10 * SKEL) ** -0.5, 0.09375, ((0, 8), (1, 4)), jnp.float32),
        "couple_third": scatter_about(keys[12], (BOXES_X, BOXES_Y, 5, SKEL, SKEL // 4), (10 * SKEL) ** -0.5, 0.09375, ((0, 8), (1, 4)), jnp.float32),
        "couple_fourth": scatter_about(keys[13], (BOXES_X, BOXES_Y, 5, SKEL, SKEL // 8), (10 * SKEL) ** -0.5, 0.09375, ((0, 8), (1, 4)), jnp.float32),
        "root_inverse": scatter_about(keys[14], (BOXES_X, BOXES_Y, SKEL, SKEL // 8), (2 * SKEL) ** -0.5, 0.21875, ((0, 8), (1, 4)), jnp.float32),
    }


HIGHEST = lax.Precision.HIGHEST
GROUPS = ((1, 1), (1, 2), (2, 2), (2, 4))
MERGE_ALONG = (1, 0, 1)


def assemble(pieces, level_index):
    if level_index == 0:
        return pieces
    total_x = pieces.shape[0]
    total_y = pieces.shape[1]
    inner_shape = tuple(pieces.shape[2:-1])
    piece_width = pieces.shape[-1]
    inner_rank = len(inner_shape)
    middle = list(range(inner_rank))
    if level_index == 1:
        blocks = pieces.reshape((total_x, total_y // 2, 2) + inner_shape + (piece_width,))
        axes_order = [0, 1] + [3 + position for position in middle] + [2, 3 + inner_rank]
        shape_out = (total_x, total_y // 2)
    elif level_index == 2:
        blocks = pieces.reshape((total_x // 2, 2, total_y // 2, 2) + inner_shape + (piece_width,))
        axes_order = [0, 2] + [4 + position for position in middle] + [1, 3, 4 + inner_rank]
        shape_out = (total_x // 2, total_y // 2)
    else:
        blocks = pieces.reshape((total_x // 2, 2, total_y // 4, 2, 2) + inner_shape + (piece_width,))
        axes_order = [0, 2] + [5 + position for position in middle] + [3, 1, 4, 5 + inner_rank]
        shape_out = (total_x // 2, total_y // 4)
    arranged = jnp.transpose(blocks, axes_order)
    return arranged.reshape(shape_out + inner_shape + (piece_width * 2 ** level_index,))


def from_lower(field, axis_number):
    padding = jnp.zeros_like(lax.slice_in_dim(field, 0, 1, axis=axis_number))
    kept = lax.slice_in_dim(field, 0, field.shape[axis_number] - 1, axis=axis_number)
    return jnp.concatenate([padding, kept], axis=axis_number)


def from_upper(field, axis_number):
    padding = jnp.zeros_like(lax.slice_in_dim(field, 0, 1, axis=axis_number))
    kept = lax.slice_in_dim(field, 1, field.shape[axis_number], axis=axis_number)
    return jnp.concatenate([kept, padding], axis=axis_number)


def reference(right_sides, skeleton_order, interp_first, interp_second, interp_third, interp_fourth,
              inverse_first, inverse_second, inverse_third, inverse_fourth,
              couple_first, couple_second, couple_third, couple_fourth, root_inverse):
    interps = (interp_first, interp_second, interp_third, interp_fourth)
    inverses = (inverse_first, inverse_second, inverse_third, inverse_fourth)
    couples = (couple_first, couple_second, couple_third, couple_fourth)
    vector = right_sides
    stored = []
    skeleton = vector
    for level_index in range(4):
        group_x, group_y = GROUPS[level_index]
        perm_grid = skeleton_order[::group_x, ::group_y, level_index]
        arranged = jnp.take_along_axis(vector, perm_grid[:, :, None, :], axis=3)
        skel_part = arranged[..., :SKEL]
        redund_part = arranged[..., SKEL:]
        interp_full = assemble(interps[level_index], level_index)
        inverse_full = assemble(inverses[level_index], level_index)
        couple_full = assemble(couples[level_index], level_index)
        lowered = redund_part - jnp.einsum("abns,absr->abnr", skel_part, interp_full, precision=HIGHEST)
        solved = jnp.einsum("abnk,abkr->abnr", lowered, inverse_full, precision=HIGHEST)
        stacked = jnp.stack([solved, from_lower(solved, 0), from_upper(solved, 0),
                             from_lower(solved, 1), from_upper(solved, 1)], axis=2)
        skeleton = skel_part - jnp.einsum("abknr,abkrs->abns", stacked, couple_full, precision=HIGHEST)
        stored.append((perm_grid, interp_full, inverse_full, couple_full, solved))
        if level_index < 3:
            if MERGE_ALONG[level_index] == 1:
                vector = jnp.concatenate([skeleton[:, 0::2], skeleton[:, 1::2]], axis=-1)
            else:
                vector = jnp.concatenate([skeleton[0::2], skeleton[1::2]], axis=-1)
    skel_value = jnp.einsum("abns,abst->abnt", skeleton, assemble(root_inverse, 3), precision=HIGHEST)
    for level_index in (3, 2, 1, 0):
        perm_grid, interp_full, inverse_full, couple_full, solved = stored[level_index]
        products = jnp.einsum("abns,abkrs->abknr", skel_value, couple_full, precision=HIGHEST)
        update = (products[:, :, 0] + from_upper(products[:, :, 1], 0) + from_lower(products[:, :, 2], 0)
                  + from_upper(products[:, :, 3], 1) + from_lower(products[:, :, 4], 1))
        redund_sol = solved - jnp.einsum("abnk,abrk->abnr", update, inverse_full, precision=HIGHEST)
        skel_sol = skel_value - jnp.einsum("abnr,absr->abns", redund_sol, interp_full, precision=HIGHEST)
        combined = jnp.concatenate([skel_sol, redund_sol], axis=-1)
        inverse_perm = jnp.argsort(perm_grid, axis=-1).astype(jnp.int32)
        vector = jnp.take_along_axis(combined, inverse_perm[:, :, None, :], axis=3)
        if level_index > 0:
            lower_half = vector[..., :SKEL]
            upper_half = vector[..., SKEL:]
            count_x, count_y, rows_count = vector.shape[0], vector.shape[1], vector.shape[2]
            if MERGE_ALONG[level_index - 1] == 1:
                skel_value = jnp.stack([lower_half, upper_half], axis=2).reshape(count_x, 2 * count_y, rows_count, SKEL)
            else:
                skel_value = jnp.stack([lower_half, upper_half], axis=1).reshape(2 * count_x, count_y, rows_count, SKEL)
    return vector
```

```python
import functools

import jax
import jax.numpy as jnp
from jax import lax
from jax.experimental import pallas as pl
from jax.experimental.pallas import tpu as pltpu
from jax.sharding import PartitionSpec as P

REACH = ((1, 1), (1, 2), (2, 2), (2, 4))
F32 = jnp.float32
BF16 = jnp.bfloat16
MESH = pl.DeviceIdType.MESH
NN = (((1,), (0,)), ((), ()))
TN = (((0,), (0,)), ((), ()))
NT = (((1,), (1,)), ((), ()))


def halves(x):
    high = x.astype(BF16)
    return high, (x - high.astype(F32)).astype(BF16)


def product(a, b, dims):
    return lax.dot_general(a, b, dims, preferred_element_type=F32)


def dot3(a, b, dims):
    ah, al = halves(a)
    bh, bl = halves(b)
    return product(ah, bh, dims) + (product(ah, bl, dims) + product(al, bh, dims))


def pick_left(onehot, b, dims):
    bh, bl = halves(b)
    return product(onehot, bh, dims) + product(onehot, bl, dims)


def flips(m):
    return (m >> 1) & 1, (m & 1) | ((m >> 2 & 1) << 1)


def kernel(size_x, size_y, *refs):
    (rhs, order_col, order_row, t0, t1, t2, t3, g0, g1, g2, g3, k0, k1, k2, k3, root, out) = refs[:17]
    (ybuf, vbuf, qsend, qrecv, urecv1, urecv2, urecv3, xrecv1, xrecv2, xrecv3, xpart, tg1, tg2, tg3,
     n0, n1, n2, n3, abuf, ypart, tpart, ssend, send, recv) = refs[17:]
    interps, inverses, couples = (t0, t1, t2, t3), (g0, g1, g2, g3), (k0, k1, k2, k3)
    urecvs = (None, urecv1, urecv2, urecv3)
    xrecvs = (None, xrecv1, xrecv2, xrecv3)
    tgs = (None, tg1, tg2, tg3)
    ns = (n0, n1, n2, n3)
    skel = t0.shape[2]
    box = 2 * skel
    i, j = lax.axis_index("bx"), lax.axis_index("by")
    bits = (lax.rem(j, 2), lax.rem(i, 2), lax.rem(lax.div(j, 2), 2))
    ranks = [jnp.int32(0), bits[0], bits[0] + 2 * bits[1], bits[0] + 2 * bits[1] + 4 * bits[2]]

    def toggled(value, mask):
        for b in (0, 1):
            if mask >> b & 1:
                value = value + (1 << b) * (1 - 2 * lax.rem(lax.div(value, 1 << b), 2))
        return value

    def member(m):
        mx, my = flips(m)
        return (toggled(i, mx), toggled(j, my))

    def rank_of(level, m):
        rank = jnp.int32(0)
        for b in range(level):
            bit = bits[b]
            rank = rank + (1 << b) * ((1 - bit) if m >> b & 1 else bit)
        return rank

    count = [0]

    def slot():
        count[0] += 1
        return count[0] - 1

    def neighbour(level, k):
        rx, ry = REACH[level]
        bx, by = lax.div(i, rx), lax.div(j, ry)
        if k == 1:
            return i >= rx, (i - rx, j)
        if k == 2:
            return i + rx < size_x, (i + rx, j)
        if k == 3:
            return j >= ry, (i, j - ry)
        return j + ry < size_y, (i, j + ry)

    opposite = {1: 2, 2: 1, 3: 4, 4: 3}
    level_has = [[k for k in (1, 2, 3, 4) if (REACH[l][0] < size_x if k < 3 else REACH[l][1] < size_y)] for l in range(4)]

    def rcopy(src, dst, s, dev):
        return pltpu.make_async_remote_copy(src, dst, send.at[s], recv.at[s], device_id=dev, device_id_type=MESH)

    for level in range(4):
        for k in (1, 2, 3, 4):
            there, _ = neighbour(level, k)

            @pl.when(jnp.logical_not(there))
            def _():
                ybuf[level, pl.ds(k * skel, skel), :] = jnp.zeros((skel, ybuf.shape[2]), F32)
                qrecv[level, k - 1] = jnp.zeros((skel, ybuf.shape[2]), F32)

    barrier = pltpu.get_barrier_semaphore()
    for m in range(1, 8):
        pl.semaphore_signal(barrier, 1, device_id=member(m), device_id_type=MESH)
    total = jnp.int32(7)
    greeted = set()
    for level in range(4):
        for k in level_has[level]:
            key = (k, REACH[level][0] if k < 3 else REACH[level][1])
            if key in greeted:
                continue
            greeted.add(key)
            there, dev = neighbour(level, k)

            @pl.when(there)
            def _():
                pl.semaphore_signal(barrier, 1, device_id=dev, device_id_type=MESH)
            total = total + there.astype(jnp.int32)
    pl.semaphore_wait(barrier, total)

    pending = []

    t_copies = [[], [], [], []]

    def send_interp(level):
        for m in range(1, 1 << level):
            c = rcopy(interps[level].at[0, 0], tgs[level].at[ranks[level]], slot(), member(m))
            c.start()
            t_copies[level].append(c)
            pending.append(c)

    send_interp(1)

    def make_n(level):
        own = inverses[level][0, 0]
        cols = own.shape[1]
        if level == 0:
            acc = dot3(interps[0][0, 0], own, NN)
        else:
            tgs[level][ranks[level]] = interps[level][0, 0]
            for c in t_copies[level]:
                c.wait_recv()
            acc = jnp.zeros((skel, cols), F32)
            for q in range(1 << level):
                acc = acc + dot3(tgs[level][q], inverses[level][0, 0, q * cols:(q + 1) * cols, :], NN)
        ns[level][:skel, :] = -acc
        ns[level][skel:, :] = own

    def onehot_pt(level):
        lanes = lax.broadcasted_iota(jnp.int32, (box, box), 1)
        return jnp.where(lanes == order_col[:, level:level + 1], 1.0, 0.0).astype(BF16)

    def onehot_p(level):
        rows = lax.broadcasted_iota(jnp.int32, (box, box), 0)
        return jnp.where(rows == order_row[0, 0, level:level + 1, :], 1.0, 0.0).astype(BF16)

    for level in range(4):
        cols = interps[level].shape[3]
        rank = ranks[level]
        rows = pl.ds(pl.multiple_of(rank * cols, cols), cols)
        make_n(level)
        if level == 0:
            abuf[...] = pick_left(onehot_pt(0), rhs[0, 0], NT)
        else:
            abuf[...] = pick_left(onehot_pt(level), vbuf[level - 1], NN)
        y_own = dot3(ns[level][...], abuf[...], TN)
        ypart[level, :cols, :] = y_own
        ybuf[level, rows, :] = y_own
        gathers = []
        for m in range(1, 1 << level):
            c = rcopy(ypart.at[level, pl.ds(0, cols), :], ybuf.at[level, rows, :], slot(), member(m))
            c.start()
            gathers.append(c)
            pending.append(c)
        for c in gathers:
            c.wait_recv()
        for k in level_has[level]:
            s = slot()
            far = opposite[k]
            there, dev = neighbour(level, k)
            c = rcopy(ybuf.at[level, pl.ds(0, skel), :], ybuf.at[level, pl.ds(far * skel, skel), :], s, dev)

            @pl.when(there)
            def _():
                c.start()
            pending.append((there, c))
        base = count[0] - len(level_has[level])
        if level < 2:
            send_interp(level + 2)
        for k in level_has[level]:
            there, dev = neighbour(level, k)
            sent_as = level_has[level].index(opposite[k])
            c = rcopy(ybuf.at[level, pl.ds(0, skel), :], ybuf.at[level, pl.ds(k * skel, skel), :], base + sent_as, dev)

            @pl.when(there)
            def _():
                c.wait_recv()
        coupling = couples[level][0, 0].reshape(5 * skel, cols)
        s_own = abuf[rows, :] - dot3(coupling, ybuf[level], TN)
        ssend[level, :cols, :] = s_own
        wide = min(level + 1, 3)
        spot = pl.ds(pl.multiple_of(ranks[wide] * cols, cols), cols)
        vbuf[level, spot, :] = s_own
        gathers = []
        for m in range(1, 1 << wide):
            c = rcopy(ssend.at[level, pl.ds(0, cols), :], vbuf.at[level, spot, :], slot(), member(m))
            c.start()
            gathers.append(c)
            pending.append(c)
        for c in gathers:
            c.wait_recv()

    t_own = dot3(root[0, 0], vbuf[3, :skel, :], TN)

    for level in (3, 2, 1, 0):
        cols = interps[level].shape[3]
        rank = ranks[level]
        members = 1 << level
        rows = pl.ds(pl.multiple_of(rank * cols, cols), cols)
        tpart[:cols, :] = t_own
        q = dot3(couples[level][0, 0].reshape(5 * skel, cols), t_own, NN)
        qsend[level] = q
        base = count[0]
        for k in level_has[level]:
            s = slot()
            there, dev = neighbour(level, k)
            c = rcopy(qsend.at[level, pl.ds(k * skel, skel), :], qrecv.at[level, opposite[k] - 1], s, dev)

            @pl.when(there)
            def _():
                c.start()
            pending.append((there, c))
        for k in level_has[level]:
            there, dev = neighbour(level, k)
            sent_as = level_has[level].index(opposite[k])
            c = rcopy(qsend.at[level, pl.ds(k * skel, skel), :], qrecv.at[level, k - 1], base + sent_as, dev)

            @pl.when(there)
            def _():
                c.wait_recv()
        u = q[:skel] + ((qrecv[level, 0] + qrecv[level, 1]) + (qrecv[level, 2] + qrecv[level, 3]))
        if level > 0:
            qsend[level, :skel, :] = u
            gathers = []
            for m in range(1, members):
                far_rows = pl.ds(pl.multiple_of(rank_of(level, m) * cols, cols), cols)
                c = rcopy(qsend.at[level, far_rows, :], urecvs[level].at[m - 1], slot(), member(m))
                c.start()
                gathers.append(c)
                pending.append(c)
            for c in gathers:
                c.wait_recv()
            u_own = qsend[level, rows, :]
            for m in range(1, members):
                u_own = u_own + urecvs[level][m - 1]
        else:
            u_own = u
        y_own = ypart[level, :cols, :]
        comb = -dot3(ns[level][...], u_own, NN)
        low = dot3(interps[level][0, 0], y_own, NN)
        abuf[:skel, :] = comb[:skel] - low
        abuf[skel:, :] = comb[skel:]
        abuf[rows, :] = abuf[rows, :] + t_own
        rows_y = pl.ds(pl.multiple_of(skel + rank * cols, 8), cols)
        abuf[rows_y, :] = abuf[rows_y, :] + y_own
        if level > 0:
            xpart[level] = pick_left(onehot_p(level), abuf[...], NN)
            size = box // members
            gathers = []
            for m in range(1, members):
                far_rows = pl.ds(pl.multiple_of(rank_of(level, m) * size, size), size)
                c = rcopy(xpart.at[level, far_rows, :], xrecvs[level].at[m - 1], slot(), member(m))
                c.start()
                gathers.append(c)
                pending.append(c)
            for c in gathers:
                c.wait_recv()
            t_own = xpart[level, pl.ds(pl.multiple_of(rank * size, size), size), :]
            for m in range(1, members):
                t_own = t_own + xrecvs[level][m - 1]
        else:
            ch, cl = halves(abuf[...])
            pt = onehot_pt(0)
            out[0, 0] = product(ch, pt, TN) + product(cl, pt, TN)

    for item in pending:
        if isinstance(item, tuple):
            there, c = item

            @pl.when(there)
            def _():
                c.wait_send()
        else:
            item.wait_send()


def body(size_x, size_y, right_sides, skeleton_order, *weights):
    rows = right_sides.shape[2]
    box = right_sides.shape[3]
    skel = box // 2
    order_col = skeleton_order[0, 0].T
    vm = lambda *shape: pltpu.VMEM(shape, F32)
    widths = [w.shape[3] for w in weights[:4]]
    scratch = [
        vm(4, 5 * skel, rows), vm(4, box, rows), vm(4, 5 * skel, rows), vm(4, 4, skel, rows),
        vm(1, widths[1], rows), vm(3, widths[2], rows), vm(7, widths[3], rows),
        vm(1, box // 2, rows), vm(3, box // 4, rows), vm(7, box // 8, rows),
        vm(4, box, rows),
        vm(2, skel, widths[1]), vm(4, skel, widths[2]), vm(8, skel, widths[3]),
        vm(box, widths[0]), vm(box, widths[1]), vm(box, widths[2]), vm(box, widths[3]),
        vm(box, rows), vm(4, skel, rows), vm(skel, rows), vm(4, skel, rows),
        pltpu.SemaphoreType.DMA((128,)), pltpu.SemaphoreType.DMA((128,)),
    ]
    return pl.pallas_call(
        functools.partial(kernel, size_x, size_y),
        out_shape=jax.ShapeDtypeStruct(right_sides.shape, F32),
        in_specs=[pl.BlockSpec(memory_space=pltpu.VMEM)] * (3 + len(weights)),
        out_specs=pl.BlockSpec(memory_space=pltpu.VMEM),
        scratch_shapes=scratch,
        compiler_params=pltpu.CompilerParams(
            collective_id=0, has_side_effects=True, vmem_limit_bytes=60 * 2**20
        ),
    )(right_sides, order_col, skeleton_order, *weights)


def solution(mesh):
    four = P("bx", "by", None, None)
    five = P("bx", "by", None, None, None)
    in_specs = (four,) * 10 + (five,) * 4 + (four,)
    return jax.shard_map(
        functools.partial(body, mesh.shape["bx"], mesh.shape["by"]),
        mesh=mesh, in_specs=in_specs, out_specs=four, check_vma=False,
    )
```

```python
import functools

import jax
import jax.numpy as jnp
from jax import lax
from jax.experimental import pallas as pl
from jax.experimental.pallas import tpu as pltpu
from jax.sharding import PartitionSpec as P

REACH = ((1, 1), (1, 2), (2, 2), (2, 4))
F32 = jnp.float32
BF16 = jnp.bfloat16
MESH = pl.DeviceIdType.MESH
NN = (((1,), (0,)), ((), ()))
TN = (((0,), (0,)), ((), ()))
NT = (((1,), (1,)), ((), ()))


def halves(x):
    high = x.astype(BF16)
    return high, (x - high.astype(F32)).astype(BF16)


def product(a, b, dims):
    return lax.dot_general(a, b, dims, preferred_element_type=F32)


def dot3(a, b, dims):
    ah, al = halves(a)
    bh, bl = halves(b)
    return product(ah, bh, dims) + (product(ah, bl, dims) + product(al, bh, dims))


def pick_left(onehot, b, dims):
    bh, bl = halves(b)
    return product(onehot, bh, dims) + product(onehot, bl, dims)


def flips(m):
    return (m >> 1) & 1, (m & 1) | ((m >> 2 & 1) << 1)


def kernel(size_x, size_y, *refs):
    (rhs, order_col, order_row, t0, t1, t2, t3, g0, g1, g2, g3, k0, k1, k2, k3, root, out) = refs[:17]
    (ybuf, vbuf, qsend, qrecv, urecv1, urecv2, urecv3, xrecv1, xrecv2, xrecv3, xpart, tg1, tg2, tg3,
     n0, n1, n2, n3, abuf, ypart, tpart, ssend, ptbuf, send, recv) = refs[17:]
    interps, inverses, couples = (t0, t1, t2, t3), (g0, g1, g2, g3), (k0, k1, k2, k3)
    urecvs = (None, urecv1, urecv2, urecv3)
    xrecvs = (None, xrecv1, xrecv2, xrecv3)
    tgs = (None, tg1, tg2, tg3)
    ns = (n0, n1, n2, n3)
    skel = t0.shape[2]
    box = 2 * skel
    i, j = lax.axis_index("bx"), lax.axis_index("by")
    bits = (lax.rem(j, 2), lax.rem(i, 2), lax.rem(lax.div(j, 2), 2))
    ranks = [jnp.int32(0), bits[0], bits[0] + 2 * bits[1], bits[0] + 2 * bits[1] + 4 * bits[2]]

    def toggled(value, mask):
        for b in (0, 1):
            if mask >> b & 1:
                value = value + (1 << b) * (1 - 2 * lax.rem(lax.div(value, 1 << b), 2))
        return value

    def member(m):
        mx, my = flips(m)
        return (toggled(i, mx), toggled(j, my))

    def rank_of(level, m):
        rank = jnp.int32(0)
        for b in range(level):
            bit = bits[b]
            rank = rank + (1 << b) * ((1 - bit) if m >> b & 1 else bit)
        return rank

    count = [0]

    def slot():
        count[0] += 1
        return count[0] - 1

    def neighbour(level, k):
        rx, ry = REACH[level]
        bx, by = lax.div(i, rx), lax.div(j, ry)
        if k == 1:
            return i >= rx, (i - rx, j)
        if k == 2:
            return i + rx < size_x, (i + rx, j)
        if k == 3:
            return j >= ry, (i, j - ry)
        return j + ry < size_y, (i, j + ry)

    opposite = {1: 2, 2: 1, 3: 4, 4: 3}
    level_has = [[k for k in (1, 2, 3, 4) if (REACH[l][0] < size_x if k < 3 else REACH[l][1] < size_y)] for l in range(4)]

    def rcopy(src, dst, s, dev):
        return pltpu.make_async_remote_copy(src, dst, send.at[s], recv.at[s], device_id=dev, device_id_type=MESH)

    for level in range(4):
        for k in (1, 2, 3, 4):
            there, _ = neighbour(level, k)

            @pl.when(jnp.logical_not(there))
            def _():
                ybuf[level, pl.ds(k * skel, skel), :] = jnp.zeros((skel, ybuf.shape[2]), F32)
                qrecv[level, k - 1] = jnp.zeros((skel, ybuf.shape[2]), F32)

    barrier = pltpu.get_barrier_semaphore()
    for m in range(1, 8):
        pl.semaphore_signal(barrier, 1, device_id=member(m), device_id_type=MESH)
    total = jnp.int32(7)
    greeted = set()
    for level in range(4):
        for k in level_has[level]:
            key = (k, REACH[level][0] if k < 3 else REACH[level][1])
            if key in greeted:
                continue
            greeted.add(key)
            there, dev = neighbour(level, k)

            @pl.when(there)
            def _():
                pl.semaphore_signal(barrier, 1, device_id=dev, device_id_type=MESH)
            total = total + there.astype(jnp.int32)
    pl.semaphore_wait(barrier, total)

    pending = []

    t_copies = [[], [], [], []]

    def send_interp(level):
        for m in [m for m in range(1, 1 << level) if not m & 2]:
            c = rcopy(interps[level].at[0, 0], tgs[level].at[ranks[level]], slot(), member(m))
            c.start()
            t_copies[level].append(c)
            pending.append(c)

    send_interp(1)

    def make_n(level):
        own = inverses[level][0, 0]
        cols = own.shape[1]
        if level == 0:
            acc = dot3(interps[0][0, 0], own, NN)
        else:
            tgs[level][ranks[level]] = interps[level][0, 0]
            for c in t_copies[level]:
                c.wait_recv()
            shared = []
            for m in [m for m in range(1 << level) if not m & 2 and level > 1]:
                block = rank_of(level, m)
                held = interps[level].at[0, 0] if m == 0 else tgs[level].at[block]
                c = rcopy(held, tgs[level].at[block], slot(), member(2))
                c.start()
                shared.append(c)
                pending.append(c)
            for c in shared:
                c.wait_recv()
            acc = jnp.zeros((skel, cols), F32)
            for q in range(1 << level):
                acc = acc + dot3(tgs[level][q], inverses[level][0, 0, q * cols:(q + 1) * cols, :], NN)
        ns[level][:skel, :] = -acc
        ns[level][skel:, :] = own

    def onehot_pt(level):
        lanes = lax.broadcasted_iota(jnp.int32, (box, box), 1)
        return jnp.where(lanes == order_col[:, level:level + 1], 1.0, 0.0).astype(BF16)

    def onehot_p(level):
        rows = lax.broadcasted_iota(jnp.int32, (box, box), 0)
        return jnp.where(rows == order_row[0, 0, level:level + 1, :], 1.0, 0.0).astype(BF16)

    for level in range(4):
        cols = interps[level].shape[3]
        rank = ranks[level]
        rows = pl.ds(pl.multiple_of(rank * cols, cols), cols)
        if level == 0:
            make_n(0)
            abuf[...] = pick_left(onehot_pt(0), rhs[0, 0], NT)
        else:
            abuf[...] = pick_left(ptbuf[...], vbuf[level - 1], NN)
        y_own = dot3(ns[level][...], abuf[...], TN)
        ypart[level, :cols, :] = y_own
        ybuf[level, rows, :] = y_own
        gathers = []
        for m in range(1, 1 << level):
            c = rcopy(ypart.at[level, pl.ds(0, cols), :], ybuf.at[level, rows, :], slot(), member(m))
            c.start()
            gathers.append(c)
            pending.append(c)
        for c in gathers:
            c.wait_recv()
        for k in level_has[level]:
            s = slot()
            far = opposite[k]
            there, dev = neighbour(level, k)
            c = rcopy(ybuf.at[level, pl.ds(0, skel), :], ybuf.at[level, pl.ds(far * skel, skel), :], s, dev)

            @pl.when(there)
            def _():
                c.start()
            pending.append((there, c))
        base = count[0] - len(level_has[level])
        if level < 2:
            send_interp(level + 2)
        if level < 3:
            make_n(level + 1)
            ptbuf[...] = onehot_pt(level + 1)
        for k in level_has[level]:
            there, dev = neighbour(level, k)
            sent_as = level_has[level].index(opposite[k])
            c = rcopy(ybuf.at[level, pl.ds(0, skel), :], ybuf.at[level, pl.ds(k * skel, skel), :], base + sent_as, dev)

            @pl.when(there)
            def _():
                c.wait_recv()
        coupling = couples[level][0, 0].reshape(5 * skel, cols)
        s_own = abuf[rows, :] - dot3(coupling, ybuf[level], TN)
        ssend[level, :cols, :] = s_own
        wide = min(level + 1, 3)
        spot = pl.ds(pl.multiple_of(ranks[wide] * cols, cols), cols)
        vbuf[level, spot, :] = s_own
        gathers = []
        for m in range(1, 1 << wide):
            c = rcopy(ssend.at[level, pl.ds(0, cols), :], vbuf.at[level, spot, :], slot(), member(m))
            c.start()
            gathers.append(c)
            pending.append(c)
        for c in gathers:
            c.wait_recv()

    t_own = dot3(root[0, 0], vbuf[3, :skel, :], TN)

    for level in (3, 2, 1, 0):
        cols = interps[level].shape[3]
        rank = ranks[level]
        members = 1 << level
        rows = pl.ds(pl.multiple_of(rank * cols, cols), cols)
        tpart[:cols, :] = t_own
        q = dot3(couples[level][0, 0].reshape(5 * skel, cols), t_own, NN)
        qsend[level] = q
        base = count[0]
        for k in level_has[level]:
            s = slot()
            there, dev = neighbour(level, k)
            c = rcopy(qsend.at[level, pl.ds(k * skel, skel), :], qrecv.at[level, opposite[k] - 1], s, dev)

            @pl.when(there)
            def _():
                c.start()
            pending.append((there, c))
        y_own = ypart[level, :cols, :]
        abuf[:skel, :] = -dot3(interps[level][0, 0], y_own, NN)
        abuf[skel:, :] = jnp.zeros_like(abuf[skel:, :])
        abuf[rows, :] = abuf[rows, :] + t_own
        rows_y = pl.ds(pl.multiple_of(skel + rank * cols, 8), cols)
        abuf[rows_y, :] = y_own
        ptbuf[...] = onehot_p(level) if level > 0 else onehot_pt(0)
        for k in level_has[level]:
            there, dev = neighbour(level, k)
            sent_as = level_has[level].index(opposite[k])
            c = rcopy(qsend.at[level, pl.ds(k * skel, skel), :], qrecv.at[level, k - 1], base + sent_as, dev)

            @pl.when(there)
            def _():
                c.wait_recv()
        u = q[:skel] + ((qrecv[level, 0] + qrecv[level, 1]) + (qrecv[level, 2] + qrecv[level, 3]))
        if level > 0:
            qsend[level, :skel, :] = u
            gathers = []
            for m in range(1, members):
                far_rows = pl.ds(pl.multiple_of(rank_of(level, m) * cols, cols), cols)
                c = rcopy(qsend.at[level, far_rows, :], urecvs[level].at[m - 1], slot(), member(m))
                c.start()
                gathers.append(c)
                pending.append(c)
            for c in gathers:
                c.wait_recv()
            u_own = qsend[level, rows, :]
            for m in range(1, members):
                u_own = u_own + urecvs[level][m - 1]
        else:
            u_own = u
        comb = -dot3(ns[level][...], u_own, NN)
        abuf[...] = abuf[...] + comb
        if level > 0:
            xpart[level] = pick_left(ptbuf[...], abuf[...], NN)
            size = box // members
            gathers = []
            for m in range(1, members):
                far_rows = pl.ds(pl.multiple_of(rank_of(level, m) * size, size), size)
                c = rcopy(xpart.at[level, far_rows, :], xrecvs[level].at[m - 1], slot(), member(m))
                c.start()
                gathers.append(c)
                pending.append(c)
            for c in gathers:
                c.wait_recv()
            t_own = xpart[level, pl.ds(pl.multiple_of(rank * size, size), size), :]
            for m in range(1, members):
                t_own = t_own + xrecvs[level][m - 1]
        else:
            ch, cl = halves(abuf[...])
            pt = ptbuf[...]
            out[0, 0] = product(ch, pt, TN) + product(cl, pt, TN)

    for item in pending:
        if isinstance(item, tuple):
            there, c = item

            @pl.when(there)
            def _():
                c.wait_send()
        else:
            item.wait_send()


def body(size_x, size_y, right_sides, skeleton_order, *weights):
    rows = right_sides.shape[2]
    box = right_sides.shape[3]
    skel = box // 2
    order_col = skeleton_order[0, 0].T
    vm = lambda *shape: pltpu.VMEM(shape, F32)
    widths = [w.shape[3] for w in weights[:4]]
    scratch = [
        vm(4, 5 * skel, rows), vm(4, box, rows), vm(4, 5 * skel, rows), vm(4, 4, skel, rows),
        vm(1, widths[1], rows), vm(3, widths[2], rows), vm(7, widths[3], rows),
        vm(1, box // 2, rows), vm(3, box // 4, rows), vm(7, box // 8, rows),
        vm(4, box, rows),
        vm(2, skel, widths[1]), vm(4, skel, widths[2]), vm(8, skel, widths[3]),
        vm(box, widths[0]), vm(box, widths[1]), vm(box, widths[2]), vm(box, widths[3]),
        vm(box, rows), vm(4, skel, rows), vm(skel, rows), vm(4, skel, rows),
        pltpu.VMEM((box, box), BF16),
        pltpu.SemaphoreType.DMA((128,)), pltpu.SemaphoreType.DMA((128,)),
    ]
    return pl.pallas_call(
        functools.partial(kernel, size_x, size_y),
        out_shape=jax.ShapeDtypeStruct(right_sides.shape, F32),
        in_specs=[pl.BlockSpec(memory_space=pltpu.VMEM)] * (3 + len(weights)),
        out_specs=pl.BlockSpec(memory_space=pltpu.VMEM),
        scratch_shapes=scratch,
        compiler_params=pltpu.CompilerParams(
            collective_id=0, has_side_effects=True, vmem_limit_bytes=60 * 2**20
        ),
    )(right_sides, order_col, skeleton_order, *weights)


def solution(mesh):
    four = P("bx", "by", None, None)
    five = P("bx", "by", None, None, None)
    in_specs = (four,) * 10 + (five,) * 4 + (four,)
    return jax.shard_map(
        functools.partial(body, mesh.shape["bx"], mesh.shape["by"]),
        mesh=mesh, in_specs=in_specs, out_specs=four, check_vma=False,
    )
```
